256 devices in a mesh: row: 16 (over z_lo, y), col: 16 (over z_hi, x, core).
Axes of the slice: x: 4, y: 4, z: 8 (z_hi: 2, z_lo: 4; z = z_hi * 4 + z_lo), core: 2. Of those that a mesh axis runs over, the one named last changes fastest.
Arguments:
- gradient: bfloat16 [512, 28672], P('col', 'row'), may hold values from -6 to 6
- basis: bfloat16 [28672, 28672], P('row', 'col'), may hold values from -0.03125 to 0.03125
- eigen: float32 [512, 28672], P('row', 'col'), may hold values from 0.2 to 5
Outputs:
- result: bfloat16 [512, 28672], P('col', 'row')
The draws below stay inside these ranges and needn't reach their ends.
All inputs are finite; a program needn't handle non-finite values.
Results may differ from the reference program's by a relative error of at most 0.0044.
Values may be sent and summed in bfloat16 or wider, within the bound.
A program may use at most 64 MiB of HBM per device.

```python
import math
import jax
import jax.numpy as jnp
from jax import lax

FF = 28672
ROWS = 512
N_COL = 16


def block_scale(key, dims, pieces, smallest, largest):
    def one(position, blocks):
        steps = jax.random.uniform(jax.random.fold_in(jax.random.fold_in(key, 6), position), (blocks,), jnp.float32, smallest / len(pieces), largest / len(pieces))
        return jnp.repeat(jnp.exp(steps), dims[position] // blocks).reshape((-1,) + (1,) * (len(dims) - position - 1))

    loudness = one(*pieces[0])
    for cut in pieces[1:]:
        loudness = loudness * one(*cut)
    return loudness


def centred(key, shape, deviation, most, split=(), kind=jnp.bfloat16):
    array = jax.random.normal(key, shape, jnp.float32) * deviation
    if len(split) > 0:
        array = block_scale(key, shape, split, -0.22, 0.18) * array
    return jnp.clip(array, min=-most, max=most).astype(kind)


def setup_inputs(seed: int = 0) -> dict:
    keys = jax.random.split(jax.random.key(seed), 4)
    return {
        "gradient": centred(keys[0], (ROWS, FF), 1.0, 6.0, ((0, 16), (1, 16))),
        "basis": centred(keys[1], (FF, FF), FF ** -0.5, 0.03125, ((0, 16), (1, 16))),
        "eigen": jnp.clip(jnp.exp(math.log(5.0) - 3.218876 * jax.random.uniform(keys[2], (ROWS, FF), jnp.float32) ** block_scale(keys[2], (ROWS, FF), ((0, 16), (1, 16)), -0.2, 0.2)), 0.2, 5.0),
    }


def reference(gradient, basis, eigen):
    width = FF // N_COL
    grad_float = gradient.astype(jnp.float32)

    def rotate_block(index):
        start = (index * width).astype(jnp.int32)
        block = lax.dynamic_slice_in_dim(basis, start, width, 1).astype(jnp.float32)
        return jnp.dot(grad_float, block, precision=lax.Precision.HIGHEST)

    blocks = lax.map(rotate_block, jnp.arange(N_COL, dtype=jnp.int32))
    rotated = jnp.concatenate([blocks[i] for i in range(N_COL)], axis=1)
    scaled = (rotated / eigen).astype(jnp.bfloat16).astype(jnp.float32)

    def back_block(index):
        start = (index * width).astype(jnp.int32)
        block = lax.dynamic_slice_in_dim(basis, start, width, 0).astype(jnp.float32)
        return jnp.dot(scaled, block.T, precision=lax.Precision.HIGHEST)

    backs = lax.map(back_block, jnp.arange(N_COL, dtype=jnp.int32))
    result = jnp.concatenate([backs[i] for i in range(N_COL)], axis=1)
    return result.astype(jnp.bfloat16)
```

```python
import functools

import jax
import jax.numpy as jnp
from jax import lax
from jax.experimental import pallas as pl
from jax.experimental.pallas import tpu as pltpu
from jax.sharding import PartitionSpec as P

MESH = pl.DeviceIdType.MESH
HALVES = 2
TILES = 2
NSEM = 192


def kernel(g_ref, b_ref, e_ref, out_ref, basis, eigen, g_all, part, ysend, yrecv, ysum, zsend, zrecv, s_all,
           back, crecv, xsum, xsend, xrecv, tsend, trecv, tsum, ssem, rsem, lsem):
    f32, bf16 = jnp.float32, jnp.bfloat16
    cols = basis.shape[1]
    hr = g_all.shape[2]
    tw = cols // TILES
    r, c = lax.axis_index("row"), lax.axis_index("col")
    z, y = r // 4, r % 4
    zh, x, k = c // 8, (c // 2) % 4, c % 2

    def row_dev(dz, dy):
        return (((z + dz) % 4) * 4 + (y + dy) % 4, c)

    def col_dev(dzh, dx, dk):
        return (r, ((zh + dzh) % 2) * 8 + ((x + dx) % 4) * 2 + (k + dk) % 2)

    def col_id(dzh, dx, dk):
        return ((zh + dzh) % 2) * 8 + ((x + dx) % 4) * 2 + (k + dk) % 2

    count = [0]
    started = []

    def send(src, dst, device):
        i = count[0]
        count[0] += 1
        copy = pltpu.make_async_remote_copy(
            src_ref=src, dst_ref=dst, send_sem=ssem.at[i], recv_sem=rsem.at[i],
            device_id=device, device_id_type=MESH)
        copy.start()
        started.append(copy)
        return copy

    local = [
        pltpu.make_async_copy(b_ref, basis, lsem.at[0]),
        pltpu.make_async_copy(e_ref, eigen, lsem.at[1]),
    ]
    for h in range(HALVES):
        local.append(pltpu.make_async_copy(g_ref.at[pl.ds(h * hr, hr)], g_all.at[h, c], lsem.at[2 + h]))
    for copy in local:
        copy.start()

    barrier = pltpu.get_barrier_semaphore()
    peers = [row_dev(0, 1), row_dev(0, 3), row_dev(1, 0), row_dev(2, 0), row_dev(3, 0),
             col_dev(1, 0, 0), col_dev(0, 1, 0), col_dev(0, 2, 0), col_dev(0, 3, 0), col_dev(0, 0, 1)]
    for peer in peers:
        pl.semaphore_signal(barrier, inc=1, device_id=peer, device_id_type=MESH)
    pl.semaphore_wait(barrier, len(peers))

    spread = {}

    def spread_own(h):
        own = g_ref.at[pl.ds(h * hr, hr)]
        there = g_all.at[h, c]
        spread[h, "z"] = send(own, there, col_dev(1, 0, 0))
        for dx in (1, 3, 2):
            spread[h, "x", dx] = send(own, there, col_dev(0, dx, 0))
        spread[h, "s"] = [send(own, there, col_dev(0, 0, 1))]

    def to_sibling(h, j):
        spread[h, "s"].append(send(g_all.at[h, j], g_all.at[h, j], col_dev(0, 0, 1)))

    def spread_far(h):
        spread[h, "z"].wait_recv()
        j = col_id(1, 0, 0)
        for dx in (1, 3, 2):
            spread[h, "zx", dx] = send(g_all.at[h, j], g_all.at[h, j], col_dev(0, dx, 0))
        to_sibling(h, j)

    def spread_near(h):
        for far, name in ((0, "x"), (1, "zx")):
            for dx in (1, 3, 2):
                spread[h, name, dx].wait_recv()
                to_sibling(h, col_id(far, 4 - dx, 0))

    def spread_end(h):
        for copy in spread[h, "s"]:
            copy.wait_recv()
        local[2 + h].wait()

    ring = {}

    def product(h, t):
        lhs = g_all[h].reshape(-1, cols)
        p = jnp.dot(lhs, basis[:, pl.ds(t * tw, tw)], preferred_element_type=f32)
        part[h, t] = p.reshape(4, 4, hr, tw)

    def y_first(h, t):
        p = part.at[h, t]
        up, down, across = (y + 1) % 4, (y + 3) % 4, (y + 2) % 4
        sb, rb = ysend.at[h, t], yrecv.at[h, t]
        for i, (zs, d, dy) in enumerate(((0, across, 1), (2, across, 3), (2, up, 1), (0, down, 3))):
            for q in range(2):
                sb[i, q] = p[zs + q, d].astype(bf16)
            ring[h, t, i] = send(sb.at[i], rb.at[i], row_dev(0, dy))

    def y_second(h, t):
        p = part.at[h, t]
        sb, rb = ysend.at[h, t], yrecv.at[h, t]
        for i, (zs, dy) in enumerate(((0, 1), (2, 3))):
            ring[h, t, i].wait_recv()
            d = (y + dy) % 4
            for q in range(2):
                sb[4 + i, q] = (p[zs + q, d] + rb[i, q].astype(f32)).astype(bf16)
            ring[h, t, 4 + i] = send(sb.at[4 + i], rb.at[4 + i], row_dev(0, dy))

    def y_end(h, t):
        p = part.at[h, t]
        rb = yrecv.at[h, t]
        for i in (2, 3, 4, 5):
            ring[h, t, i].wait_recv()
        for q in range(2):
            ysum[h, t, q] = p[q, y] + rb[3, q].astype(f32) + rb[4, q].astype(f32)
            ysum[h, t, 2 + q] = p[2 + q, y] + rb[2, q].astype(f32) + rb[5, q].astype(f32)
        for dz in (1, 2, 3):
            zsend[h, t, dz - 1] = ysum[h, t, (z + dz) % 4].astype(bf16)
            ring[h, t, "z", dz] = send(zsend.at[h, t, dz - 1], zrecv.at[h, t, dz - 1], row_dev(dz, 0))

    def tile_of(h, t, i):
        return s_all.at[h, i, :, pl.ds(t * tw, tw)]

    def y_spread(h, t, dz):
        at = tile_of(h, t, ((z + 4 - dz) % 4) * 4 + y)
        for dy in (1, 3):
            ring[h, t, "sy", dz, dy] = send(at, at, row_dev(0, dy))

    def z_end(h, t):
        total = ysum[h, t, z]
        for dz in (1, 2, 3):
            ring[h, t, "z", dz].wait_recv()
            total = total + zrecv[h, t, dz - 1].astype(f32)
        scaled = total / eigen[pl.ds(h * hr, hr), pl.ds(t * tw, tw)]
        s_all[h, r, :, pl.ds(t * tw, tw)] = scaled.astype(bf16)
        at = tile_of(h, t, r)
        for dz in (1, 2, 3):
            ring[h, t, "sz", dz] = send(at, at, row_dev(dz, 0))
        y_spread(h, t, 0)

    def z_spread(h, t):
        for dz in (1, 3, 2):
            ring[h, t, "sz", dz].wait_recv()
            y_spread(h, t, dz)

    def y_relay(h, t):
        for dz in (0, 1, 3, 2):
            dy = 1 if dz < 2 else 3
            ring[h, t, "sy", dz, dy].wait_recv()
            at = tile_of(h, t, ((z + 4 - dz) % 4) * 4 + (y + 4 - dy) % 4)
            ring[h, t, "sr", dz] = send(at, at, row_dev(0, dy))

    def s_end(h):
        for t in range(TILES):
            for dz in range(4):
                ring[h, t, "sy", dz, 3 if dz < 2 else 1].wait_recv()
                ring[h, t, "sr", dz].wait_recv()

    def product_back(h, t):
        lhs = s_all[h].reshape(-1, cols)
        q = lax.dot_general(lhs, basis[pl.ds(t * tw, tw), :], (((1,), (1,)), ((), ())), preferred_element_type=f32)
        back[h, t] = q.reshape(8, 2, hr, tw)
        ring[h, t, "c"] = send(back.at[h, t, :, (k + 1) % 2], crecv.at[h, t], col_dev(0, 0, 1))

    def core_end(h, t):
        ring[h, t, "c"].wait_recv()
        for far in range(2):
            for q in range(4):
                xsum[h, t, far, q] = back[h, t, far * 4 + q, k] + crecv[h, t, far * 4 + q]
        for dx in (1, 3, 2):
            for far in range(2):
                xsend[h, t, dx - 1, far] = xsum[h, t, far, (x + dx) % 4].astype(bf16)
            ring[h, t, "x", dx] = send(xsend.at[h, t, dx - 1], xrecv.at[h, t, dx - 1], col_dev(0, dx, 0))

    def x_end(h, t):
        for dx in (1, 3, 2):
            ring[h, t, "x", dx].wait_recv()
        for far in range(2):
            total = xsum[h, t, far, x]
            for dx in (1, 2, 3):
                total = total + xrecv[h, t, dx - 1, far].astype(f32)
            tsum[h, t, far] = total
        tsend[h, t] = tsum[h, t, (zh + 1) % 2].astype(bf16)
        ring[h, t, "t"] = send(tsend.at[h, t], trecv.at[h, t], col_dev(1, 0, 0))

    def finish(h, t):
        ring[h, t, "t"].wait_recv()
        total = tsum[h, t, zh] + trecv[h, t].astype(f32)
        out_ref[pl.ds(h * hr, hr), pl.ds(t * tw, tw)] = total.astype(bf16)

    spread_own(0)
    spread_far(0)
    spread_own(1)
    spread_near(0)
    spread_end(0)
    local[0].wait()
    product(0, 0)
    y_first(0, 0)
    spread_far(1)
    product(0, 1)
    y_first(0, 1)
    y_second(0, 0)
    spread_near(1)
    y_second(0, 1)
    spread_end(1)
    product(1, 0)
    y_first(1, 0)
    y_end(0, 0)
    product(1, 1)
    y_first(1, 1)
    local[1].wait()
    y_end(0, 1)
    y_second(1, 0)
    z_end(0, 0)
    y_second(1, 1)
    z_end(0, 1)
    z_spread(0, 0)
    y_end(1, 0)
    z_spread(0, 1)
    y_end(1, 1)
    y_relay(0, 0)
    z_end(1, 0)
    y_relay(0, 1)
    z_end(1, 1)
    z_spread(1, 0)
    z_spread(1, 1)
    s_end(0)
    product_back(0, 0)
    y_relay(1, 0)
    product_back(0, 1)
    y_relay(1, 1)
    core_end(0, 0)
    core_end(0, 1)
    x_end(0, 0)
    x_end(0, 1)
    s_end(1)
    product_back(1, 0)
    product_back(1, 1)
    core_end(1, 0)
    core_end(1, 1)
    finish(0, 0)
    finish(0, 1)
    x_end(1, 0)
    x_end(1, 1)
    finish(1, 0)
    finish(1, 1)
    for copy in started:
        copy.wait_send()


def per_device(gradient, basis, eigen):
    rows, cols = gradient.shape
    hr, tw = rows // HALVES, cols // TILES
    f32, bf16 = jnp.float32, jnp.bfloat16
    ht = (HALVES, TILES)
    any_space = pl.BlockSpec(memory_space=pl.ANY)
    return pl.pallas_call(
        kernel,
        out_shape=jax.ShapeDtypeStruct((rows, cols), bf16),
        in_specs=[any_space] * 3,
        out_specs=pl.BlockSpec(memory_space=pltpu.VMEM),
        scratch_shapes=[
            pltpu.VMEM(basis.shape, bf16),
            pltpu.VMEM(eigen.shape, f32),
            pltpu.VMEM((HALVES, 16, hr, cols), bf16),
            pltpu.VMEM((*ht, 4, 4, hr, tw), f32),
            pltpu.VMEM((*ht, 6, 2, hr, tw), bf16),
            pltpu.VMEM((*ht, 6, 2, hr, tw), bf16),
            pltpu.VMEM((*ht, 4, hr, tw), f32),
            pltpu.VMEM((*ht, 3, hr, tw), bf16),
            pltpu.VMEM((*ht, 3, hr, tw), bf16),
            pltpu.VMEM((HALVES, 16, hr, cols), bf16),
            pltpu.VMEM((*ht, 8, 2, hr, tw), f32),
            pltpu.VMEM((*ht, 8, hr, tw), f32),
            pltpu.VMEM((*ht, 2, 4, hr, tw), f32),
            pltpu.VMEM((*ht, 3, 2, hr, tw), bf16),
            pltpu.VMEM((*ht, 3, 2, hr, tw), bf16),
            pltpu.VMEM((*ht, hr, tw), bf16),
            pltpu.VMEM((*ht, hr, tw), bf16),
            pltpu.VMEM((*ht, 2, hr, tw), f32),
            pltpu.SemaphoreType.DMA((NSEM,)),
            pltpu.SemaphoreType.DMA((NSEM,)),
            pltpu.SemaphoreType.DMA((4,)),
        ],
        compiler_params=pltpu.CompilerParams(
            collective_id=0, has_side_effects=True, vmem_limit_bytes=60 << 20),
    )(gradient, basis, eigen)


def solution(mesh):
    return jax.shard_map(
        per_device,
        mesh=mesh,
        in_specs=(P("col", "row"), P("row", "col"), P("row", "col")),
        out_specs=P("col", "row"),
        check_vma=False,
    )
```

```python
import functools

import jax
import jax.numpy as jnp
from jax import lax
from jax.experimental import pallas as pl
from jax.experimental.pallas import tpu as pltpu
from jax.sharding import PartitionSpec as P

MESH = pl.DeviceIdType.MESH
HALVES = 2
LANES = (7, 7)
TILES = len(LANES)
NSEM = 186


def kernel(g_ref, b_ref, e_ref, out_ref, basis, eigen, g_all, part, ysend, yrecv, ysum, zsend, zrecv, s_all,
           back, crecv, xsum, xsend, xrecv, tsend, trecv, ssem, rsem, lsem):
    f32, bf16 = jnp.float32, jnp.bfloat16
    cols = basis.shape[1]
    hr = g_all.shape[3]
    step = cols // sum(LANES)
    tiles = [pl.ds(sum(LANES[:t]) * step, LANES[t] * step) for t in range(TILES)]
    r, c = lax.axis_index("row"), lax.axis_index("col")
    z, y = r // 4, r % 4
    zh, x, k = c // 8, (c // 2) % 4, c % 2

    def row_dev(dz, dy):
        return (((z + dz) % 4) * 4 + (y + dy) % 4, c)

    def col_dev(dzh, dx, dk):
        return (r, ((zh + dzh) % 2) * 8 + ((x + dx) % 4) * 2 + (k + dk) % 2)

    started = []

    def send(src, dst, device):
        i = len(started)
        copy = pltpu.make_async_remote_copy(
            src_ref=src, dst_ref=dst, send_sem=ssem.at[i], recv_sem=rsem.at[i],
            device_id=device, device_id_type=MESH)
        copy.start()
        started.append(copy)
        return copy

    local = [pltpu.make_async_copy(g_ref.at[pl.ds(h * hr, hr)], g_all.at[h, zh, c % 8], lsem.at[2 + h]) for h in range(HALVES)]
    local += [pltpu.make_async_copy(e_ref, eigen, lsem.at[1]), pltpu.make_async_copy(b_ref, basis, lsem.at[0])]
    for copy in local:
        copy.start()

    barrier = pltpu.get_barrier_semaphore()
    peers = [row_dev(0, 1), row_dev(0, 3), row_dev(1, 0), row_dev(2, 0), row_dev(3, 0),
             col_dev(1, 0, 0), col_dev(0, 1, 0), col_dev(0, 2, 0), col_dev(0, 3, 0), col_dev(0, 0, 1)]
    for peer in peers:
        pl.semaphore_signal(barrier, inc=1, device_id=peer, device_id_type=MESH)
    pl.semaphore_wait(barrier, len(peers))

    ring = {}
    seen = set()

    def once(copy):
        if id(copy) not in seen:
            seen.add(id(copy))
            copy.wait()

    def own(h):
        mine, there = g_ref.at[pl.ds(h * hr, hr)], g_all.at[h, zh, c % 8]
        for dx in (1, 3, 2):
            ring["x", h, 0, dx] = send(mine, there, col_dev(0, dx, 0))
        ring["s", h, 0, 0] = send(mine, there, col_dev(0, 0, 1))
        ring["z", h] = send(mine, there, col_dev(1, 0, 0))

    def far(h):
        ring["z", h].wait_recv()
        at = g_all.at[h, (zh + 1) % 2, c % 8]
        for dx in (1, 3, 2):
            ring["x", h, 1, dx] = send(at, at, col_dev(0, dx, 0))
        ring["s", h, 1, 0] = send(at, at, col_dev(0, 0, 1))

    def near(h, u, dx):
        ring["x", h, u, dx].wait_recv()
        at = g_all.at[h, (zh + u) % 2, ((x + 4 - dx) % 4) * 2 + k]
        ring["s", h, u, dx] = send(at, at, col_dev(0, 0, 1))

    def product(h, u, t):
        if t == 0:
            for i in range(4):
                ring["s", h, u, i].wait_recv()
            if u == 0:
                once(local[h])
        once(local[HALVES + 1])
        lhs = g_all[h, (zh + u) % 2].reshape(-1, cols)
        p = jnp.dot(lhs, basis[:, tiles[t]], preferred_element_type=f32)
        part[h, u, t] = p.reshape(2, 4, hr, -1)
        up, down, across = (y + 1) % 4, (y + 3) % 4, (y + 2) % 4
        for i, (q, d, dy) in enumerate(((0, across, 1), (1, across, 3), (1, up, 1), (0, down, 3))):
            ysend[h, u, t, i] = part[h, u, t, q, d].astype(bf16)
            ring["r", h, u, t, i] = send(ysend.at[h, u, t, i], yrecv.at[h, u, t, i], row_dev(0, dy))

    def y_second(h, u, t, q):
        dy = 1 + 2 * q
        ring["r", h, u, t, q].wait_recv()
        ysend[h, u, t, 4 + q] = (
            part[h, u, t, q, (y + dy) % 4] + yrecv[h, u, t, q].astype(f32)).astype(bf16)
        ring["r", h, u, t, 4 + q] = send(
            ysend.at[h, u, t, 4 + q], yrecv.at[h, u, t, 4 + q], row_dev(0, dy))

    def y_end(h, u, t):
        for i in (2, 3, 4, 5):
            ring["r", h, u, t, i].wait_recv()
        for q in range(2):
            ysum[h, t, ((zh + u) % 2) * 2 + q] = (
                part[h, u, t, q, y] + yrecv[h, u, t, 3 - q].astype(f32)
                + yrecv[h, u, t, 4 + q].astype(f32))

    def z_first(h, t):
        for dz in (2, 1, 3):
            zsend[h, t, dz - 1] = ysum[h, t, (z + dz) % 4].astype(bf16)
            ring["zr", h, t, dz] = send(
                zsend.at[h, t, dz - 1], zrecv.at[h, t, dz - 1], row_dev(dz, 0))

    def tile_of(h, t, z1, y1):
        return s_all.at[h, z1 // 2, (z1 % 2) * 4 + y1, :, tiles[t]]

    def y_spread(h, t, dz):
        at = tile_of(h, t, (z + 4 - dz) % 4, y)
        for dy in (1, 3):
            ring["sy", h, t, dz, dy] = send(at, at, row_dev(0, dy))

    def z_end(h, t):
        once(local[HALVES])
        total = ysum[h, t, z]
        for dz in (1, 2, 3):
            ring["zr", h, t, dz].wait_recv()
            total = total + zrecv[h, t, dz - 1].astype(f32)
        scaled = total / eigen[pl.ds(h * hr, hr), tiles[t]]
        s_all[h, z // 2, (z % 2) * 4 + y, :, tiles[t]] = scaled.astype(bf16)
        at = tile_of(h, t, z, y)
        for dz in (2, 1, 3):
            ring["sz", h, t, dz] = send(at, at, row_dev(dz, 0))
        y_spread(h, t, 0)

    def z_spread(h, t, dz):
        ring["sz", h, t, dz].wait_recv()
        y_spread(h, t, dz)

    def y_relay(h, t, dz):
        dy = 1 if dz < 2 else 3
        ring["sy", h, t, dz, dy].wait_recv()
        at = tile_of(h, t, (z + 4 - dz) % 4, (y + 4 - dy) % 4)
        ring["sr", h, t, dz] = send(at, at, row_dev(0, dy))

    def s_end(h):
        if ("end", h) not in seen:
            seen.add(("end", h))
            for t in range(TILES):
                for dz in range(4):
                    ring["sy", h, t, dz, 3 if dz < 2 else 1].wait_recv()
                    ring["sr", h, t, dz].wait_recv()

    def product_back(h, u, t):
        s_end(h)
        lhs = s_all[h, (zh + u) % 2].reshape(-1, cols)
        q = lax.dot_general(lhs, basis[tiles[t], :], (((1,), (1,)), ((), ())), preferred_element_type=f32)
        back[h, u, t] = q.reshape(4, 2, hr, -1)
        ring["c", h, u, t] = send(
            back.at[h, u, t, :, (k + 1) % 2], crecv.at[h, u, t], col_dev(0, 0, 1))

    def core_end(h, u, t):
        ring["c", h, u, t].wait_recv()
        for dx in (1, 3, 2, 0):
            to = (x + dx) % 4
            total = back[h, u, t, to, k] + crecv[h, u, t, to]
            if dx == 0:
                xsum[h, u, t] = total
            else:
                xsend[h, u, t, dx - 1] = total.astype(bf16)
                ring["rx", h, u, t, dx] = send(
                    xsend.at[h, u, t, dx - 1], xrecv.at[h, u, t, dx - 1], col_dev(0, dx, 0))

    def x_end(h, u, t):
        total = xsum[h, u, t]
        for dx in (1, 3, 2):
            ring["rx", h, u, t, dx].wait_recv()
            total = total + xrecv[h, u, t, dx - 1].astype(f32)
        if u == 1:
            tsend[h, t] = total.astype(bf16)
            ring["t", h, t] = send(tsend.at[h, t], trecv.at[h, t], col_dev(1, 0, 0))
        else:
            ring["t", h, t].wait_recv()
            total = total + trecv[h, t].astype(f32)
            out_ref[pl.ds(h * hr, hr), tiles[t]] = total.astype(bf16)

    own(0)
    near(0, 0, 1)
    near(0, 0, 3)
    near(0, 0, 2)
    own(1)
    product(0, 0, 0)
    far(0)
    product(0, 0, 1)
    near(1, 0, 1)
    near(1, 0, 3)
    near(1, 0, 2)
    y_second(0, 0, 0, 0)
    y_second(0, 0, 0, 1)
    y_second(0, 0, 1, 0)
    y_second(0, 0, 1, 1)
    product(1, 0, 0)
    far(1)
    near(0, 1, 1)
    near(0, 1, 3)
    near(0, 1, 2)
    y_end(0, 0, 0)
    product(1, 0, 1)
    y_end(0, 0, 1)
    y_second(1, 0, 0, 0)
    product(0, 1, 0)
    y_second(1, 0, 0, 1)
    y_second(1, 0, 1, 0)
    y_second(1, 0, 1, 1)
    near(1, 1, 1)
    near(1, 1, 3)
    near(1, 1, 2)
    product(0, 1, 1)
    y_second(0, 1, 0, 0)
    y_second(0, 1, 0, 1)
    y_end(1, 0, 0)
    y_second(0, 1, 1, 0)
    y_second(0, 1, 1, 1)
    y_end(1, 0, 1)
    y_end(0, 1, 0)
    z_first(0, 0)
    product(1, 1, 0)
    y_end(0, 1, 1)
    z_first(0, 1)
    product(1, 1, 1)
    y_second(1, 1, 0, 0)
    y_second(1, 1, 0, 1)
    y_second(1, 1, 1, 0)
    y_second(1, 1, 1, 1)
    z_end(0, 0)
    z_end(0, 1)
    y_end(1, 1, 0)
    z_first(1, 0)
    z_spread(0, 0, 1)
    z_spread(0, 0, 3)
    z_spread(0, 0, 2)
    y_end(1, 1, 1)
    z_first(1, 1)
    z_spread(0, 1, 1)
    z_spread(0, 1, 3)
    z_spread(0, 1, 2)
    y_relay(0, 0, 0)
    y_relay(0, 0, 1)
    y_relay(0, 0, 3)
    y_relay(0, 0, 2)
    y_relay(0, 1, 0)
    z_end(1, 0)
    y_relay(0, 1, 1)
    y_relay(0, 1, 3)
    y_relay(0, 1, 2)
    z_end(1, 1)
    z_spread(1, 0, 1)
    z_spread(1, 0, 3)
    z_spread(1, 0, 2)
    z_spread(1, 1, 1)
    z_spread(1, 1, 3)
    z_spread(1, 1, 2)
    product_back(0, 1, 0)
    y_relay(1, 0, 0)
    y_relay(1, 0, 1)
    y_relay(1, 0, 3)
    y_relay(1, 0, 2)
    product_back(0, 1, 1)
    y_relay(1, 1, 0)
    y_relay(1, 1, 1)
    y_relay(1, 1, 3)
    y_relay(1, 1, 2)
    product_back(0, 0, 0)
    core_end(0, 1, 0)
    product_back(0, 0, 1)
    core_end(0, 1, 1)
    core_end(0, 0, 0)
    product_back(1, 1, 0)
    product_back(1, 1, 1)
    core_end(1, 1, 0)
    product_back(1, 0, 0)
    core_end(1, 1, 1)
    product_back(1, 0, 1)
    core_end(0, 0, 1)
    x_end(0, 1, 0)
    x_end(0, 1, 1)
    core_end(1, 0, 0)
    core_end(1, 0, 1)
    x_end(1, 1, 0)
    x_end(1, 1, 1)
    x_end(0, 0, 0)
    x_end(0, 0, 1)
    x_end(1, 0, 0)
    x_end(1, 0, 1)
    for copy in started:
        copy.wait_send()


def per_device(gradient, basis, eigen):
    rows, cols = gradient.shape
    hr, tw = rows // HALVES, cols // TILES
    ht, hut = (HALVES, TILES), (HALVES, 2, TILES)
    f32, bf16 = jnp.float32, jnp.bfloat16
    any_space = pl.BlockSpec(memory_space=pl.ANY)
    return pl.pallas_call(
        kernel,
        out_shape=jax.ShapeDtypeStruct((rows, cols), bf16),
        in_specs=[any_space] * 3,
        out_specs=pl.BlockSpec(memory_space=pltpu.VMEM),
        scratch_shapes=[
            pltpu.VMEM(basis.shape, bf16),
            pltpu.VMEM(eigen.shape, f32),
            pltpu.VMEM((HALVES, 2, 8, hr, cols), bf16),
            pltpu.VMEM((*hut, 2, 4, hr, tw), f32),
            pltpu.VMEM((*hut, 6, hr, tw), bf16),
            pltpu.VMEM((*hut, 6, hr, tw), bf16),
            pltpu.VMEM((*ht, 4, hr, tw), f32),
            pltpu.VMEM((*ht, 3, hr, tw), bf16),
            pltpu.VMEM((*ht, 3, hr, tw), bf16),
            pltpu.VMEM((HALVES, 2, 8, hr, cols), bf16),
            pltpu.VMEM((*hut, 4, 2, hr, tw), f32),
            pltpu.VMEM((*hut, 4, hr, tw), f32),
            pltpu.VMEM((*hut, hr, tw), f32),
            pltpu.VMEM((*hut, 3, hr, tw), bf16),
            pltpu.VMEM((*hut, 3, hr, tw), bf16),
            pltpu.VMEM((*ht, hr, tw), bf16),
            pltpu.VMEM((*ht, hr, tw), bf16),
            pltpu.SemaphoreType.DMA((NSEM,)),
            pltpu.SemaphoreType.DMA((NSEM,)),
            pltpu.SemaphoreType.DMA((2 + HALVES,)),
        ],
        compiler_params=pltpu.CompilerParams(
            collective_id=0, has_side_effects=True, vmem_limit_bytes=60 << 20),
    )(gradient, basis, eigen)


def solution(mesh):
    return jax.shard_map(
        per_device,
        mesh=mesh,
        in_specs=(P("col", "row"), P("row", "col"), P("row", "col")),
        out_specs=P("col", "row"),
        check_vma=False,
    )
```

```python
import functools

import jax
import jax.numpy as jnp
from jax import lax
from jax.experimental import pallas as pl
from jax.experimental.pallas import tpu as pltpu
from jax.sharding import PartitionSpec as P

MESH = pl.DeviceIdType.MESH
HALVES = 2
LANES = (7, 7)
TILES = len(LANES)
NSEM = 186


def kernel(g_ref, b_ref, e_ref, out_ref, basis, eigen, g_all, part, ysend, yrecv, ysum, zsend, zrecv, s_all,
           back, crecv, xsum, xsend, xrecv, tsend, trecv, ssem, rsem, lsem):
    f32, bf16 = jnp.float32, jnp.bfloat16
    cols = basis.shape[1]
    hr = g_all.shape[3]
    step = cols // sum(LANES)
    tiles = [pl.ds(sum(LANES[:t]) * step, LANES[t] * step) for t in range(TILES)]
    r, c = lax.axis_index("row"), lax.axis_index("col")
    z, y = r // 4, r % 4
    zh, x, k = c // 8, (c // 2) % 4, c % 2

    def row_dev(dz, dy):
        return (((z + dz) % 4) * 4 + (y + dy) % 4, c)

    def col_dev(dzh, dx, dk):
        return (r, ((zh + dzh) % 2) * 8 + ((x + dx) % 4) * 2 + (k + dk) % 2)

    started = []

    def send(src, dst, device):
        i = len(started)
        copy = pltpu.make_async_remote_copy(
            src_ref=src, dst_ref=dst, send_sem=ssem.at[i], recv_sem=rsem.at[i],
            device_id=device, device_id_type=MESH)
        copy.start()
        started.append(copy)
        return copy

    local = [pltpu.make_async_copy(g_ref.at[pl.ds(h * hr, hr)], g_all.at[h, zh, c % 8], lsem.at[2 + h]) for h in range(HALVES)]
    local += [pltpu.make_async_copy(e_ref, eigen, lsem.at[1]), pltpu.make_async_copy(b_ref, basis, lsem.at[0])]
    for copy in local:
        copy.start()

    barrier = pltpu.get_barrier_semaphore()
    peers = [row_dev(0, 1), row_dev(0, 3), row_dev(1, 0), row_dev(2, 0), row_dev(3, 0),
             col_dev(1, 0, 0), col_dev(0, 1, 0), col_dev(0, 2, 0), col_dev(0, 3, 0), col_dev(0, 0, 1)]
    for peer in peers:
        pl.semaphore_signal(barrier, inc=1, device_id=peer, device_id_type=MESH)
    pl.semaphore_wait(barrier, len(peers))

    ring = {}
    seen = set()

    def once(copy):
        if id(copy) not in seen:
            seen.add(id(copy))
            copy.wait()

    def own(h):
        mine, there = g_ref.at[pl.ds(h * hr, hr)], g_all.at[h, zh, c % 8]
        for dx in (1, 3, 2):
            ring["x", h, 0, dx] = send(mine, there, col_dev(0, dx, 0))
        ring["s", h, 0, 0] = send(mine, there, col_dev(0, 0, 1))
        ring["z", h] = send(mine, there, col_dev(1, 0, 0))

    def far(h):
        ring["z", h].wait_recv()
        at = g_all.at[h, (zh + 1) % 2, c % 8]
        for dx in (1, 3, 2):
            ring["x", h, 1, dx] = send(at, at, col_dev(0, dx, 0))
        ring["s", h, 1, 0] = send(at, at, col_dev(0, 0, 1))

    def near(h, u, dx):
        ring["x", h, u, dx].wait_recv()
        at = g_all.at[h, (zh + u) % 2, ((x + 4 - dx) % 4) * 2 + k]
        ring["s", h, u, dx] = send(at, at, col_dev(0, 0, 1))

    def product(h, u, t):
        if t == 0:
            for i in range(4):
                ring["s", h, u, i].wait_recv()
            if u == 0:
                once(local[h])
        once(local[HALVES + 1])
        lhs = g_all[h, (zh + u) % 2].reshape(-1, cols)
        p = jnp.dot(lhs, basis[:, tiles[t]], preferred_element_type=f32)
        part[h, u, t] = p.reshape(2, 4, hr, -1)
        up, down, across = (y + 1) % 4, (y + 3) % 4, (y + 2) % 4
        for i, (q, d, dy) in enumerate(((0, across, 1), (1, across, 3), (1, up, 1), (0, down, 3))):
            ysend[h, u, t, i] = part[h, u, t, q, d].astype(bf16)
            ring["r", h, u, t, i] = send(ysend.at[h, u, t, i], yrecv.at[h, u, t, i], row_dev(0, dy))

    def y_second(h, u, t, q):
        dy = 1 + 2 * q
        ring["r", h, u, t, q].wait_recv()
        ysend[h, u, t, 4 + q] = (
            part[h, u, t, q, (y + dy) % 4] + yrecv[h, u, t, q].astype(f32)).astype(bf16)
        ring["r", h, u, t, 4 + q] = send(
            ysend.at[h, u, t, 4 + q], yrecv.at[h, u, t, 4 + q], row_dev(0, dy))

    def y_end(h, u, t):
        for i in (2, 3, 4, 5):
            ring["r", h, u, t, i].wait_recv()
        for q in range(2):
            ysum[h, t, ((zh + u) % 2) * 2 + q] = (
                part[h, u, t, q, y] + yrecv[h, u, t, 3 - q].astype(f32)
                + yrecv[h, u, t, 4 + q].astype(f32))

    def z_first(h, t):
        for dz in (2, 1, 3):
            zsend[h, t, dz - 1] = ysum[h, t, (z + dz) % 4].astype(bf16)
            ring["zr", h, t, dz] = send(
                zsend.at[h, t, dz - 1], zrecv.at[h, t, dz - 1], row_dev(dz, 0))

    def tile_of(h, t, z1, y1):
        return s_all.at[h, z1 // 2, (z1 % 2) * 4 + y1, :, tiles[t]]

    def y_spread(h, t, dz):
        at = tile_of(h, t, (z + 4 - dz) % 4, y)
        for dy in (1, 3):
            ring["sy", h, t, dz, dy] = send(at, at, row_dev(0, dy))

    def z_end(h, t):
        once(local[HALVES])
        total = ysum[h, t, z]
        for dz in (1, 2, 3):
            ring["zr", h, t, dz].wait_recv()
            total = total + zrecv[h, t, dz - 1].astype(f32)
        scaled = total / eigen[pl.ds(h * hr, hr), tiles[t]]
        s_all[h, z // 2, (z % 2) * 4 + y, :, tiles[t]] = scaled.astype(bf16)
        at = tile_of(h, t, z, y)
        for dz in (2, 1, 3):
            ring["sz", h, t, dz] = send(at, at, row_dev(dz, 0))
        y_spread(h, t, 0)

    def z_spread(h, t, dz):
        ring["sz", h, t, dz].wait_recv()
        y_spread(h, t, dz)

    def y_relay(h, t, dz):
        dy = 1 if dz < 2 else 3
        ring["sy", h, t, dz, dy].wait_recv()
        at = tile_of(h, t, (z + 4 - dz) % 4, (y + 4 - dy) % 4)
        ring["sr", h, t, dz] = send(at, at, row_dev(0, dy))

    def s_end(h):
        if ("end", h) not in seen:
            seen.add(("end", h))
            for t in range(TILES):
                for dz in range(4):
                    ring["sy", h, t, dz, 3 if dz < 2 else 1].wait_recv()
                    ring["sr", h, t, dz].wait_recv()

    def product_back(h, u, t):
        s_end(h)
        lhs = s_all[h, (zh + u) % 2].reshape(-1, cols)
        q = lax.dot_general(lhs, basis[tiles[t], :], (((1,), (1,)), ((), ())), preferred_element_type=f32)
        back[h, u, t] = q.reshape(4, 2, hr, -1)
        ring["c", h, u, t] = send(
            back.at[h, u, t, :, (k + 1) % 2], crecv.at[h, u, t], col_dev(0, 0, 1))

    def core_end(h, u, t):
        ring["c", h, u, t].wait_recv()
        for dx in (1, 3, 2, 0):
            to = (x + dx) % 4
            total = back[h, u, t, to, k] + crecv[h, u, t, to]
            if dx == 0:
                xsum[h, u, t] = total
            else:
                xsend[h, u, t, dx - 1] = total.astype(bf16)
                ring["rx", h, u, t, dx] = send(
                    xsend.at[h, u, t, dx - 1], xrecv.at[h, u, t, dx - 1], col_dev(0, dx, 0))

    def x_end(h, u, t):
        total = xsum[h, u, t]
        for dx in (1, 3, 2):
            ring["rx", h, u, t, dx].wait_recv()
            total = total + xrecv[h, u, t, dx - 1].astype(f32)
        if u == 1:
            tsend[h, t] = total.astype(bf16)
            ring["t", h, t] = send(tsend.at[h, t], trecv.at[h, t], col_dev(1, 0, 0))
        else:
            ring["t", h, t].wait_recv()
            total = total + trecv[h, t].astype(f32)
            out_ref[pl.ds(h * hr, hr), tiles[t]] = total.astype(bf16)

    own(0)
    own(1)
    near(0, 0, 1)
    near(0, 0, 3)
    near(0, 0, 2)
    far(0)
    product(0, 0, 0)
    near(1, 0, 3)
    near(1, 0, 1)
    product(0, 0, 1)
    near(1, 0, 2)
    product(1, 0, 0)
    y_second(0, 0, 0, 0)
    near(0, 1, 1)
    near(0, 1, 3)
    y_second(0, 0, 0, 1)
    far(1)
    y_second(0, 0, 1, 0)
    y_second(0, 0, 1, 1)
    near(0, 1, 2)
    product(1, 0, 1)
    product(0, 1, 0)
    y_end(0, 0, 0)
    y_second(1, 0, 0, 0)
    y_second(1, 0, 0, 1)
    product(0, 1, 1)
    y_end(0, 0, 1)
    y_second(1, 0, 1, 0)
    y_second(1, 0, 1, 1)
    near(1, 1, 1)
    near(1, 1, 3)
    near(1, 1, 2)
    y_second(0, 1, 0, 0)
    y_second(0, 1, 0, 1)
    y_end(1, 0, 0)
    y_second(0, 1, 1, 0)
    y_second(0, 1, 1, 1)
    y_end(1, 0, 1)
    y_end(0, 1, 0)
    z_first(0, 0)
    product(1, 1, 0)
    y_end(0, 1, 1)
    z_first(0, 1)
    product(1, 1, 1)
    y_second(1, 1, 0, 0)
    y_second(1, 1, 0, 1)
    y_second(1, 1, 1, 0)
    y_second(1, 1, 1, 1)
    z_end(0, 0)
    z_end(0, 1)
    y_end(1, 1, 0)
    z_first(1, 0)
    y_end(1, 1, 1)
    z_first(1, 1)
    z_spread(0, 0, 1)
    z_spread(0, 0, 3)
    z_spread(0, 0, 2)
    z_spread(0, 1, 1)
    z_spread(0, 1, 3)
    z_spread(0, 1, 2)
    y_relay(0, 0, 0)
    y_relay(0, 0, 1)
    y_relay(0, 0, 3)
    y_relay(0, 0, 2)
    y_relay(0, 1, 0)
    z_end(1, 0)
    y_relay(0, 1, 1)
    y_relay(0, 1, 3)
    y_relay(0, 1, 2)
    z_end(1, 1)
    z_spread(1, 0, 1)
    z_spread(1, 0, 3)
    z_spread(1, 0, 2)
    z_spread(1, 1, 1)
    z_spread(1, 1, 3)
    z_spread(1, 1, 2)
    product_back(0, 1, 0)
    y_relay(1, 0, 0)
    y_relay(1, 0, 1)
    y_relay(1, 0, 3)
    y_relay(1, 0, 2)
    product_back(0, 1, 1)
    y_relay(1, 1, 0)
    y_relay(1, 1, 1)
    y_relay(1, 1, 3)
    y_relay(1, 1, 2)
    product_back(0, 0, 0)
    core_end(0, 1, 0)
    product_back(0, 0, 1)
    core_end(0, 1, 1)
    core_end(0, 0, 0)
    product_back(1, 1, 0)
    product_back(1, 1, 1)
    core_end(1, 1, 0)
    product_back(1, 0, 0)
    core_end(1, 1, 1)
    product_back(1, 0, 1)
    core_end(0, 0, 1)
    x_end(0, 1, 0)
    x_end(0, 1, 1)
    core_end(1, 0, 0)
    core_end(1, 0, 1)
    x_end(1, 1, 0)
    x_end(1, 1, 1)
    x_end(0, 0, 0)
    x_end(0, 0, 1)
    x_end(1, 0, 0)
    x_end(1, 0, 1)
    for copy in started:
        copy.wait_send()


def per_device(gradient, basis, eigen):
    rows, cols = gradient.shape
    hr, tw = rows // HALVES, cols // TILES
    ht, hut = (HALVES, TILES), (HALVES, 2, TILES)
    f32, bf16 = jnp.float32, jnp.bfloat16
    any_space = pl.BlockSpec(memory_space=pl.ANY)
    return pl.pallas_call(
        kernel,
        out_shape=jax.ShapeDtypeStruct((rows, cols), bf16),
        in_specs=[any_space] * 3,
        out_specs=pl.BlockSpec(memory_space=pltpu.VMEM),
        scratch_shapes=[
            pltpu.VMEM(basis.shape, bf16),
            pltpu.VMEM(eigen.shape, f32),
            pltpu.VMEM((HALVES, 2, 8, hr, cols), bf16),
            pltpu.VMEM((*hut, 2, 4, hr, tw), f32),
            pltpu.VMEM((*hut, 6, hr, tw), bf16),
            pltpu.VMEM((*hut, 6, hr, tw), bf16),
            pltpu.VMEM((*ht, 4, hr, tw), f32),
            pltpu.VMEM((*ht, 3, hr, tw), bf16),
            pltpu.VMEM((*ht, 3, hr, tw), bf16),
            pltpu.VMEM((HALVES, 2, 8, hr, cols), bf16),
            pltpu.VMEM((*hut, 4, 2, hr, tw), f32),
            pltpu.VMEM((*hut, 4, hr, tw), f32),
            pltpu.VMEM((*hut, hr, tw), f32),
            pltpu.VMEM((*hut, 3, hr, tw), bf16),
            pltpu.VMEM((*hut, 3, hr, tw), bf16),
            pltpu.VMEM((*ht, hr, tw), bf16),
            pltpu.VMEM((*ht, hr, tw), bf16),
            pltpu.SemaphoreType.DMA((NSEM,)),
            pltpu.SemaphoreType.DMA((NSEM,)),
            pltpu.SemaphoreType.DMA((2 + HALVES,)),
        ],
        compiler_params=pltpu.CompilerParams(
            collective_id=0, has_side_effects=True, vmem_limit_bytes=60 << 20),
    )(gradient, basis, eigen)


def solution(mesh):
    return jax.shard_map(
        per_device,
        mesh=mesh,
        in_specs=(P("col", "row"), P("row", "col"), P("row", "col")),
        out_specs=P("col", "row"),
        check_vma=False,
    )
```

```python
import functools

import jax
import jax.numpy as jnp
from jax import lax
from jax.experimental import pallas as pl
from jax.experimental.pallas import tpu as pltpu
from jax.sharding import PartitionSpec as P

MESH = pl.DeviceIdType.MESH
HALVES = 2
LANES = (7, 7)
TILES = len(LANES)
NSEM = 186


def kernel(g_ref, b_ref, e_ref, out_ref, basis, eigen, g_all, part, ysend, yrecv, ysum, zsend, zrecv, s_all,
           back, crecv, xsum, xsend, xrecv, tsend, trecv, ssem, rsem, lsem):
    f32, bf16 = jnp.float32, jnp.bfloat16
    cols = basis.shape[1]
    hr = g_all.shape[3]
    step = cols // sum(LANES)
    tiles = [pl.ds(sum(LANES[:t]) * step, LANES[t] * step) for t in range(TILES)]
    r, c = lax.axis_index("row"), lax.axis_index("col")
    z, y = r // 4, r % 4
    zh, x, k = c // 8, (c // 2) % 4, c % 2

    def row_dev(dz, dy):
        return (((z + dz) % 4) * 4 + (y + dy) % 4, c)

    def col_dev(dzh, dx, dk):
        return (r, ((zh + dzh) % 2) * 8 + ((x + dx) % 4) * 2 + (k + dk) % 2)

    started = []

    def send(src, dst, device):
        i = len(started)
        copy = pltpu.make_async_remote_copy(
            src_ref=src, dst_ref=dst, send_sem=ssem.at[i], recv_sem=rsem.at[i],
            device_id=device, device_id_type=MESH)
        copy.start()
        started.append(copy)
        return copy

    local = [pltpu.make_async_copy(g_ref.at[pl.ds(h * hr, hr)], g_all.at[h, zh, c % 8], lsem.at[2 + h]) for h in range(HALVES)]
    local += [pltpu.make_async_copy(e_ref, eigen, lsem.at[1]), pltpu.make_async_copy(b_ref, basis, lsem.at[0])]
    for copy in local:
        copy.start()

    barrier = pltpu.get_barrier_semaphore()
    peers = [row_dev(0, 1), row_dev(0, 3), row_dev(1, 0), row_dev(2, 0), row_dev(3, 0),
             col_dev(1, 0, 0), col_dev(0, 1, 0), col_dev(0, 2, 0), col_dev(0, 3, 0), col_dev(0, 0, 1)]
    for peer in peers:
        pl.semaphore_signal(barrier, inc=1, device_id=peer, device_id_type=MESH)
    pl.semaphore_wait(barrier, len(peers))

    ring = {}
    seen = set()

    def once(copy):
        if id(copy) not in seen:
            seen.add(id(copy))
            copy.wait()

    def own(h):
        mine, there = g_ref.at[pl.ds(h * hr, hr)], g_all.at[h, zh, c % 8]
        for dx in (2, 1, 3):
            ring["x", h, 0, dx] = send(mine, there, col_dev(0, dx, 0))
        ring["s", h, 0, 0] = send(mine, there, col_dev(0, 0, 1))
        ring["z", h] = send(mine, there, col_dev(1, 0, 0))

    def far(h):
        ring["z", h].wait_recv()
        at = g_all.at[h, (zh + 1) % 2, c % 8]
        for dx in (2, 1, 3):
            ring["x", h, 1, dx] = send(at, at, col_dev(0, dx, 0))
        ring["s", h, 1, 0] = send(at, at, col_dev(0, 0, 1))

    def near(h, u, dx):
        ring["x", h, u, dx].wait_recv()
        at = g_all.at[h, (zh + u) % 2, ((x + 4 - dx) % 4) * 2 + k]
        ring["s", h, u, dx] = send(at, at, col_dev(0, 0, 1))

    def product(h, u, t):
        if t == 0:
            for i in range(4):
                ring["s", h, u, i].wait_recv()
            if u == 0:
                once(local[h])
        once(local[HALVES + 1])
        lhs = g_all[h, (zh + u) % 2].reshape(-1, cols)
        p = jnp.dot(lhs, basis[:, tiles[t]], preferred_element_type=f32)
        part[h, u, t] = p.reshape(2, 4, hr, -1)
        up, down, across = (y + 1) % 4, (y + 3) % 4, (y + 2) % 4
        for i, (q, d, dy) in enumerate(((0, across, 1), (1, across, 3), (1, up, 1), (0, down, 3))):
            ysend[h, u, t, i] = part[h, u, t, q, d].astype(bf16)
            ring["r", h, u, t, i] = send(ysend.at[h, u, t, i], yrecv.at[h, u, t, i], row_dev(0, dy))

    def y_second(h, u, t, q):
        dy = 1 + 2 * q
        ring["r", h, u, t, q].wait_recv()
        ysend[h, u, t, 4 + q] = (
            part[h, u, t, q, (y + dy) % 4] + yrecv[h, u, t, q].astype(f32)).astype(bf16)
        ring["r", h, u, t, 4 + q] = send(
            ysend.at[h, u, t, 4 + q], yrecv.at[h, u, t, 4 + q], row_dev(0, dy))

    def y_end(h, u, t):
        for i in (2, 3, 4, 5):
            ring["r", h, u, t, i].wait_recv()
        for q in range(2):
            ysum[h, t, ((zh + u) % 2) * 2 + q] = (
                part[h, u, t, q, y] + yrecv[h, u, t, 3 - q].astype(f32)
                + yrecv[h, u, t, 4 + q].astype(f32))

    def z_first(h, t):
        for dz in (2, 1, 3):
            zsend[h, t, dz - 1] = ysum[h, t, (z + dz) % 4].astype(bf16)
            ring["zr", h, t, dz] = send(
                zsend.at[h, t, dz - 1], zrecv.at[h, t, dz - 1], row_dev(dz, 0))

    def tile_of(h, t, z1, y1):
        return s_all.at[h, z1 // 2, (z1 % 2) * 4 + y1, :, tiles[t]]

    def y_spread(h, t, dz):
        at = tile_of(h, t, (z + 4 - dz) % 4, y)
        for dy in (1, 3):
            ring["sy", h, t, dz, dy] = send(at, at, row_dev(0, dy))

    def z_end(h, t):
        once(local[HALVES])
        total = ysum[h, t, z]
        for dz in (1, 2, 3):
            ring["zr", h, t, dz].wait_recv()
            total = total + zrecv[h, t, dz - 1].astype(f32)
        scaled = total / eigen[pl.ds(h * hr, hr), tiles[t]]
        s_all[h, z // 2, (z % 2) * 4 + y, :, tiles[t]] = scaled.astype(bf16)
        at = tile_of(h, t, z, y)
        for dz in (2, 1, 3):
            ring["sz", h, t, dz] = send(at, at, row_dev(dz, 0))
        y_spread(h, t, 0)

    def z_spread(h, t, dz):
        ring["sz", h, t, dz].wait_recv()
        y_spread(h, t, dz)

    def y_relay(h, t, dz):
        dy = 1 if dz < 2 else 3
        ring["sy", h, t, dz, dy].wait_recv()
        at = tile_of(h, t, (z + 4 - dz) % 4, (y + 4 - dy) % 4)
        ring["sr", h, t, dz] = send(at, at, row_dev(0, dy))

    def s_end(h):
        if ("end", h) not in seen:
            seen.add(("end", h))
            for t in range(TILES):
                for dz in range(4):
                    ring["sy", h, t, dz, 3 if dz < 2 else 1].wait_recv()
                    ring["sr", h, t, dz].wait_recv()

    def product_back(h, u, t):
        s_end(h)
        lhs = s_all[h, (zh + u) % 2].reshape(-1, cols)
        q = lax.dot_general(lhs, basis[tiles[t], :], (((1,), (1,)), ((), ())), preferred_element_type=f32)
        back[h, u, t] = q.reshape(4, 2, hr, -1)
        ring["c", h, u, t] = send(
            back.at[h, u, t, :, (k + 1) % 2], crecv.at[h, u, t], col_dev(0, 0, 1))

    def core_end(h, u, t):
        ring["c", h, u, t].wait_recv()
        for dx in (2, 1, 3, 0):
            to = (x + dx) % 4
            total = back[h, u, t, to, k] + crecv[h, u, t, to]
            if dx == 0:
                xsum[h, u, t] = total
            else:
                xsend[h, u, t, dx - 1] = total.astype(bf16)
                ring["rx", h, u, t, dx] = send(
                    xsend.at[h, u, t, dx - 1], xrecv.at[h, u, t, dx - 1], col_dev(0, dx, 0))

    def x_end(h, u, t):
        total = xsum[h, u, t]
        for dx in (2, 1, 3):
            ring["rx", h, u, t, dx].wait_recv()
            total = total + xrecv[h, u, t, dx - 1].astype(f32)
        if u == 1:
            tsend[h, t] = total.astype(bf16)
            ring["t", h, t] = send(tsend.at[h, t], trecv.at[h, t], col_dev(1, 0, 0))
        else:
            ring["t", h, t].wait_recv()
            total = total + trecv[h, t].astype(f32)
            out_ref[pl.ds(h * hr, hr), tiles[t]] = total.astype(bf16)

    own(0)
    own(1)
    near(0, 0, 2)
    near(0, 0, 1)
    near(0, 0, 3)
    far(0)
    product(0, 0, 0)
    near(1, 0, 1)
    near(1, 0, 2)
    product(0, 0, 1)
    near(1, 0, 3)
    product(1, 0, 0)
    y_second(0, 0, 0, 0)
    near(0, 1, 2)
    near(0, 1, 1)
    y_second(0, 0, 0, 1)
    far(1)
    y_second(0, 0, 1, 0)
    y_second(0, 0, 1, 1)
    near(0, 1, 3)
    product(1, 0, 1)
    product(0, 1, 0)
    y_end(0, 0, 0)
    y_second(1, 0, 0, 0)
    y_second(1, 0, 0, 1)
    product(0, 1, 1)
    y_end(0, 0, 1)
    y_second(1, 0, 1, 0)
    y_second(1, 0, 1, 1)
    near(1, 1, 2)
    near(1, 1, 1)
    near(1, 1, 3)
    y_second(0, 1, 0, 0)
    y_second(0, 1, 0, 1)
    y_end(1, 0, 0)
    y_second(0, 1, 1, 0)
    y_second(0, 1, 1, 1)
    y_end(1, 0, 1)
    y_end(0, 1, 0)
    z_first(0, 0)
    product(1, 1, 0)
    y_end(0, 1, 1)
    z_first(0, 1)
    product(1, 1, 1)
    y_second(1, 1, 0, 0)
    y_second(1, 1, 0, 1)
    y_second(1, 1, 1, 0)
    y_second(1, 1, 1, 1)
    z_end(0, 0)
    z_end(0, 1)
    y_end(1, 1, 0)
    z_first(1, 0)
    y_end(1, 1, 1)
    z_first(1, 1)
    z_spread(0, 0, 1)
    z_spread(0, 0, 3)
    z_spread(0, 0, 2)
    z_spread(0, 1, 1)
    z_spread(0, 1, 3)
    z_spread(0, 1, 2)
    y_relay(0, 0, 0)
    y_relay(0, 0, 1)
    y_relay(0, 0, 3)
    y_relay(0, 0, 2)
    y_relay(0, 1, 0)
    z_end(1, 0)
    y_relay(0, 1, 1)
    y_relay(0, 1, 3)
    y_relay(0, 1, 2)
    z_end(1, 1)
    z_spread(1, 0, 1)
    z_spread(1, 0, 3)
    z_spread(1, 0, 2)
    z_spread(1, 1, 1)
    z_spread(1, 1, 3)
    z_spread(1, 1, 2)
    product_back(0, 1, 0)
    y_relay(1, 0, 0)
    y_relay(1, 0, 1)
    y_relay(1, 0, 3)
    y_relay(1, 0, 2)
    product_back(0, 1, 1)
    y_relay(1, 1, 0)
    y_relay(1, 1, 1)
    y_relay(1, 1, 3)
    y_relay(1, 1, 2)
    product_back(0, 0, 0)
    core_end(0, 1, 0)
    product_back(0, 0, 1)
    core_end(0, 1, 1)
    core_end(0, 0, 0)
    product_back(1, 1, 0)
    product_back(1, 1, 1)
    core_end(1, 1, 0)
    product_back(1, 0, 0)
    core_end(1, 1, 1)
    product_back(1, 0, 1)
    core_end(0, 0, 1)
    x_end(0, 1, 0)
    x_end(0, 1, 1)
    core_end(1, 0, 0)
    core_end(1, 0, 1)
    x_end(1, 1, 0)
    x_end(1, 1, 1)
    x_end(0, 0, 0)
    x_end(0, 0, 1)
    x_end(1, 0, 0)
    x_end(1, 0, 1)
    for copy in started:
        copy.wait_send()


def per_device(gradient, basis, eigen):
    rows, cols = gradient.shape
    hr, tw = rows // HALVES, cols // TILES
    ht, hut = (HALVES, TILES), (HALVES, 2, TILES)
    f32, bf16 = jnp.float32, jnp.bfloat16
    any_space = pl.BlockSpec(memory_space=pl.ANY)
    return pl.pallas_call(
        kernel,
        out_shape=jax.ShapeDtypeStruct((rows, cols), bf16),
        in_specs=[any_space] * 3,
        out_specs=pl.BlockSpec(memory_space=pltpu.VMEM),
        scratch_shapes=[
            pltpu.VMEM(basis.shape, bf16),
            pltpu.VMEM(eigen.shape, f32),
            pltpu.VMEM((HALVES, 2, 8, hr, cols), bf16),
            pltpu.VMEM((*hut, 2, 4, hr, tw), f32),
            pltpu.VMEM((*hut, 6, hr, tw), bf16),
            pltpu.VMEM((*hut, 6, hr, tw), bf16),
            pltpu.VMEM((*ht, 4, hr, tw), f32),
            pltpu.VMEM((*ht, 3, hr, tw), bf16),
            pltpu.VMEM((*ht, 3, hr, tw), bf16),
            pltpu.VMEM((HALVES, 2, 8, hr, cols), bf16),
            pltpu.VMEM((*hut, 4, 2, hr, tw), f32),
            pltpu.VMEM((*hut, 4, hr, tw), f32),
            pltpu.VMEM((*hut, hr, tw), f32),
            pltpu.VMEM((*hut, 3, hr, tw), bf16),
            pltpu.VMEM((*hut, 3, hr, tw), bf16),
            pltpu.VMEM((*ht, hr, tw), bf16),
            pltpu.VMEM((*ht, hr, tw), bf16),
            pltpu.SemaphoreType.DMA((NSEM,)),
            pltpu.SemaphoreType.DMA((NSEM,)),
            pltpu.SemaphoreType.DMA((2 + HALVES,)),
        ],
        compiler_params=pltpu.CompilerParams(
            collective_id=0, has_side_effects=True, vmem_limit_bytes=60 << 20),
    )(gradient, basis, eigen)


def solution(mesh):
    return jax.shard_map(
        per_device,
        mesh=mesh,
        in_specs=(P("col", "row"), P("row", "col"), P("row", "col")),
        out_specs=P("col", "row"),
        check_vma=False,
    )
```
